32 devices in a mesh: inp: 8 (over y, x, core), tim: 4 (over z).
Axes of the slice: x: 2, y: 2, z: 4, core: 2. Of those that a mesh axis runs over, the one named last changes fastest.
Arguments:
- voltages: bfloat16 [2, 1024, 8192], P(None, 'inp', 'tim'), may hold values from -6 to 6
- fir_taps: int32 [4, 512], replicated, may hold values from -2048 to 2047
- station_flags: int32 [512, 4], P('inp', 'tim'), may hold values 0 or 1
- tile_pairs: int32 [528, 2], replicated, may hold values from 0 to 31, as said below
Outputs:
- visibilities: float32 [512, 528, 2, 1024], P(('inp', 'tim'))
The draws below stay inside these ranges and needn't reach their ends.
Inputs may be any that keep to these rules, and one draw needn't show every extreme that they name: `tile_pairs`: each row holds tile indices I <= J, every such pair of the 32 blocks appears exactly once, in an order drawn from the seed.
All inputs are finite; a program needn't handle non-finite values. No bound on the sum of `station_flags` on one device may be relied on, other than what follows from the above.
Results may differ from the reference program's by a relative error of at most 0.004.
Values may be sent and summed in bfloat16 or wider, within the bound.
No kernel may reach another device: no remote copies, remote signals or barrier semaphores. Data moves between devices by JAX's collectives and lax.ppermute only.
A program may use at most 256 MiB of HBM per device.

```python
import math
import jax
import jax.numpy as jnp
import numpy as np
from jax import lax

NI = 1024
NCH = 512
TAPS = 4
TB = 32
FLAGRUN = 4
SPECTRA = 16
NSAMP = 8192
NST = 512
NB = 32
NTILES = 528


def draw_tile_pairs(key, part):
    rows, cols = np.triu_indices(NB)
    table = jnp.asarray(np.stack([rows, cols], axis=-1).astype(np.int32))
    order = jax.random.permutation(key, NTILES)
    return table[order]


def place_ends(entries, rng, smallest, high):
    dims = entries.shape
    index_at = [jax.random.randint(jax.random.fold_in(rng, axis), (), 0, dims[axis]) for axis in range(len(dims))]
    entries = entries.at[tuple(index_at)].set(smallest)
    longest = dims.index(max(dims))
    index_at[longest] = (index_at[longest] + 1) % dims[longest]
    return entries.at[tuple(index_at)].set(high)


def block_scale(rng, shape, cuts, low, largest):
    def one(dim, parts):
        steps = jax.random.uniform(jax.random.fold_in(jax.random.fold_in(rng, 6), dim), (parts,), jnp.float32, low / len(cuts), largest / len(cuts))
        return jnp.repeat(jnp.exp(steps), shape[dim] // parts).reshape((-1,) + (1,) * (len(shape) - dim - 1))

    factor_of = one(*cuts[0])
    for cut in cuts[1:]:
        factor_of = factor_of * one(*cut)
    return factor_of


def scatter_about(rng, extent, spread, reach, split=(), held_as=jnp.bfloat16):
    result = spread * jax.random.normal(rng, extent, jnp.float32)
    if split:
        result = result * block_scale(rng, extent, split, -0.22, 0.18)
    return jnp.clip(result, -reach, reach).astype(held_as)


def setup_inputs(seed: int = 0) -> dict:
    arg_keys = jax.random.split(jax.random.key(seed), 5)
    voltages = scatter_about(arg_keys[0], (2, NI, NSAMP), 1.0, 6.0, ((1, 8), (2, 4)))
    fir_taps = place_ends(jax.random.randint(arg_keys[1], (TAPS, NCH), -2048, 2048), jax.random.fold_in(arg_keys[1], 1), -2048, 2047).astype(jnp.int32)
    station_flags = place_ends((jax.random.randint(arg_keys[2], (NST, SPECTRA // FLAGRUN), 0, 4) < 3).astype(jnp.int32), jax.random.fold_in(arg_keys[2], 1), 0, 1)
    tile_pairs = draw_tile_pairs(jax.random.fold_in(arg_keys[4], 71), 0)
    return dict(voltages=voltages, fir_taps=fir_taps, station_flags=station_flags, tile_pairs=tile_pairs)


def channelize(block_index, voltages, coeffs, flags):
    start = block_index * TB
    block = lax.dynamic_slice_in_dim(voltages, start, TB, 1)
    frames = block.astype(jnp.float32).reshape(2, TB, SPECTRA, NCH)
    padded = jnp.pad(frames, ((0, 0), (0, 0), (TAPS - 1, 0), (0, 0)))
    filtered = jnp.zeros_like(frames)
    for offset in range(TAPS):
        begin = TAPS - 1 - offset
        filtered = filtered + coeffs[offset] * padded[:, :, begin:begin + SPECTRA, :]
    spectrum = jnp.fft.fft(filtered[0] + 1j * filtered[1], axis=-1)
    flag_rows = lax.dynamic_slice_in_dim(flags, block_index * (TB // 2), TB // 2, 0)
    flag_full = jnp.repeat(jnp.repeat(flag_rows, 2, axis=0), FLAGRUN, axis=1).astype(jnp.bfloat16)
    real_part = jnp.real(spectrum).astype(jnp.bfloat16) * flag_full[:, :, None]
    imag_part = jnp.imag(spectrum).astype(jnp.bfloat16) * flag_full[:, :, None]
    stacked = jnp.stack([real_part, imag_part], axis=0)
    return jnp.transpose(stacked, (3, 0, 1, 2))

def reference(voltages, fir_taps, station_flags, tile_pairs):
    coeffs = fir_taps.astype(jnp.float32) * (1.0 / (2048.0 * math.sqrt(TAPS * NCH)))
    block_ids = jnp.arange(NB, dtype=jnp.int32)
    channelized = lax.map(lambda number: channelize(number, voltages, coeffs, station_flags), block_ids)
    scale = 1.0 / SPECTRA

    def correlate(channel):
        plane = lax.dynamic_index_in_dim(channelized, channel, 1, keepdims=False)
        first = jnp.take(plane, tile_pairs[:, 0], axis=0).astype(jnp.float32)
        second = jnp.take(plane, tile_pairs[:, 1], axis=0).astype(jnp.float32)
        products = jnp.einsum('gpas,gqbs->gpqab', first, second, precision=lax.Precision.HIGHEST)
        real_part = products[:, 0, 0] + products[:, 1, 1]
        imag_part = products[:, 1, 0] - products[:, 0, 1]
        return (jnp.stack([real_part, imag_part], axis=1) * scale).reshape(NTILES, 2, TB * TB)
    return lax.map(correlate, jnp.arange(NCH, dtype=jnp.int32))
```

```python
import functools
import math

import jax
import jax.numpy as jnp
import numpy as np
from jax import lax
from jax.experimental import pallas as pl
from jax.experimental.pallas import tpu as pltpu
from jax.sharding import PartitionSpec as P

TB = 32
FLAGRUN = 4
LANES = 128
PACK = LANES // TB
ROWS = TB // PACK


def shifted(block, axis, distance):
    devices = range(lax.axis_size(axis))
    route = [(i - distance, i) for i in devices if i - distance in devices]
    return lax.ppermute(block, axis, route)


def split_terms(value):
    high = value.astype(jnp.bfloat16)
    return high, (value - high.astype(jnp.float32)).astype(jnp.bfloat16)


def transform_tables(chans):
    radix = chans // LANES
    k = np.arange(LANES)
    tables = []
    for q in range(radix):
        phase = np.outer(radix * k + q, np.arange(LANES)) % chans
        angle = 2.0 * np.pi * phase / chans
        cosine, sine = np.cos(angle), np.sin(angle)
        tables.append(np.block([[cosine, sine], [-sine, cosine]]))
    table = np.stack(tables)
    high = table.astype(jnp.bfloat16)
    low = (table - high.astype(np.float64)).astype(jnp.bfloat16)
    return high, low


def channelize_kernel(volt_ref, halo_ref, taps_ref, flags_ref, high_ref, low_ref, out_ref, rows_ref, *, taps, chans):
    width = volt_ref.shape[1]
    spectra = volt_ref.shape[2] // chans
    radix = chans // LANES
    scale = 1.0 / (2048.0 * math.sqrt(taps * chans))
    coeffs = taps_ref[...].astype(jnp.float32) * scale

    def frame(part, index):
        if index < taps - 1:
            return halo_ref[part, :, index * chans : (index + 1) * chans].astype(jnp.float32)
        begin = (index - taps + 1) * chans
        return volt_ref[part, :, begin : begin + chans].astype(jnp.float32)

    folded = [[] for _ in range(radix)]
    for s in range(spectra):
        flag = flags_ref[:, s : s + 1]
        parts = []
        for part in range(2):
            total = coeffs[0:1] * frame(part, s + taps - 1)
            for p in range(1, taps):
                total = total + coeffs[p : p + 1] * frame(part, s + taps - 1 - p)
            total = total * flag
            parts.append([total[:, m * LANES : (m + 1) * LANES] for m in range(radix)])
        (r0, r1, r2, r3), (i0, i1, i2, i3) = parts
        re_even, re_odd, re_diff, re_cross = r0 + r2, r1 + r3, r0 - r2, r1 - r3
        im_even, im_odd, im_diff, im_cross = i0 + i2, i1 + i3, i0 - i2, i1 - i3
        sums = [
            (re_even + re_odd, im_even + im_odd),
            (re_diff + im_cross, im_diff - re_cross),
            (re_even - re_odd, im_even - im_odd),
            (re_diff - im_cross, im_diff + re_cross),
        ]
        for q in range(radix):
            folded[q].append(jnp.concatenate(sums[q], axis=1))
    nt = (((1,), (1,)), ((), ()))
    dot = functools.partial(lax.dot_general, dimension_numbers=nt, preferred_element_type=jnp.float32)
    for q in range(radix):
        high, low = split_terms(jnp.concatenate(folded[q], axis=0))
        result = dot(high_ref[q], high) + (dot(low_ref[q], high) + dot(high_ref[q], low))
        for part in range(2):
            for s in range(spectra):
                first = (q * 2 + part) * spectra + s
                rows_ref[pl.ds(first, LANES, stride=radix * 2 * spectra), :] = result[
                    part * LANES : (part + 1) * LANES, s * width : (s + 1) * width
                ]
    out_ref[...] = rows_ref[...].astype(jnp.bfloat16).reshape(out_ref.shape)


def channelize(voltages, halo, fir_taps, flags):
    taps, chans = fir_taps.shape
    width = voltages.shape[1]
    spectra = voltages.shape[2] // chans
    high, low = transform_tables(chans)
    return pl.pallas_call(
        functools.partial(channelize_kernel, taps=taps, chans=chans),
        out_shape=jax.ShapeDtypeStruct((chans, 2 * spectra, width), jnp.bfloat16),
        scratch_shapes=[pltpu.VMEM((chans * 2 * spectra, width), jnp.float32)],
        compiler_params=pltpu.CompilerParams(vmem_limit_bytes=40 << 20),
        name="channelize",
    )(voltages, halo, fir_taps, flags, jnp.asarray(high), jnp.asarray(low))


def correlate_kernel(place_ref, x_ref, pick_ref, spread_ref, out_ref, left_ref, right_ref, *, n_inputs, n_times):
    half = x_ref.shape[2] // 2
    width = x_ref.shape[3]
    depth = n_times * 2 * half
    deep = PACK * depth
    tiles = width // TB
    blocks = n_inputs * tiles
    row_block = lax.broadcasted_iota(jnp.int32, (deep, width), 0) // depth
    own = lax.broadcasted_iota(jnp.int32, (deep, width), 1) % PACK == row_block
    wide = tiles * LANES
    row_wide = lax.broadcasted_iota(jnp.int32, (deep, wide), 0) // depth
    own_wide = lax.broadcasted_iota(jnp.int32, (deep, wide), 1) // TB % PACK == row_wide
    sign = jnp.where(lax.broadcasted_iota(jnp.int32, (2 * half, width), 0) < half, 1.0, -1.0)
    zero = jnp.zeros((), jnp.float32)
    for i in range(n_inputs):
        plain, turned = [], []
        for t in range(n_times):
            value = x_ref[i * n_times + t, 0].astype(jnp.float32)
            plain.append(value)
            turned.append(pltpu.roll(value, half, 0) * sign)
        plain = jnp.concatenate(plain, axis=0)
        turned = jnp.concatenate(turned, axis=0)
        lefts = jnp.concatenate(
            [
                jnp.where(own, jnp.concatenate([plain] * PACK, axis=0), zero),
                jnp.where(own, jnp.concatenate([turned] * PACK, axis=0), zero),
            ],
            axis=1,
        ).astype(jnp.bfloat16)
        left = lax.dot_general(
            pick_ref[...], lefts, (((1,), (1,)), ((), ())), preferred_element_type=jnp.float32
        )
        span = tiles * ROWS * 2
        left_ref[i * span : (i + 1) * span, :] = left.astype(jnp.bfloat16)
        repeated = jnp.dot(plain.astype(jnp.bfloat16), spread_ref[...], preferred_element_type=jnp.float32)
        right = jnp.where(own_wide, jnp.concatenate([repeated] * PACK, axis=0), zero)
        right_ref[:, i * wide : (i + 1) * wide] = right.astype(jnp.bfloat16)
    tall = ROWS * 2
    for pair in range(blocks // 2):
        count = 2 * pair + 2
        grid = jnp.dot(
            left_ref[0 : count * tall, :],
            right_ref[:, pair * 2 * LANES : (pair + 1) * 2 * LANES],
            preferred_element_type=jnp.float32,
        )
        for first in range(count):
            for side in range(2):
                second = 2 * pair + side
                if first <= second:
                    out_ref[0, place_ref[first * blocks + second]] = grid[
                        first * tall : (first + 1) * tall, side * LANES : (side + 1) * LANES
                    ]


def correlate(owned, place, n_inputs, n_times, n_tiles):
    per_device, deep_half, width = owned.shape[1:]
    half = deep_half // 2
    tiles = width // TB
    blocks = n_inputs * tiles
    total = half * n_times
    tall = ROWS * 2
    row = np.arange(tiles * tall)
    column = np.arange(width)
    member = (row // 2)[:, None] == (column // PACK)[None, :]
    pick = np.concatenate([member & (row % 2 == q)[:, None] for q in range(2)], axis=1) / total
    lane = np.arange(tiles * LANES)
    spread = (lane // LANES * TB + lane % TB)[None, :] == column[:, None]
    deep = PACK * 2 * total
    grid_spec = pltpu.PrefetchScalarGridSpec(
        num_scalar_prefetch=1,
        grid=(per_device,),
        in_specs=[
            pl.BlockSpec((n_inputs * n_times, 1, deep_half, width), lambda r, place: (0, r, 0, 0)),
            pl.BlockSpec(pick.shape, lambda r, place: (0, 0)),
            pl.BlockSpec(spread.shape, lambda r, place: (0, 0)),
        ],
        out_specs=pl.BlockSpec((1, n_tiles, tall, LANES), lambda r, place: (r, 0, 0, 0)),
        scratch_shapes=[
            pltpu.VMEM((blocks * tall, deep), jnp.bfloat16),
            pltpu.VMEM((deep, blocks * LANES), jnp.bfloat16),
        ],
    )
    return pl.pallas_call(
        functools.partial(correlate_kernel, n_inputs=n_inputs, n_times=n_times),
        grid_spec=grid_spec,
        out_shape=jax.ShapeDtypeStruct((per_device, n_tiles, tall, LANES), jnp.float32),
        compiler_params=pltpu.CompilerParams(vmem_limit_bytes=48 << 20),
        name="correlate",
    )(place, owned, jnp.asarray(pick, jnp.bfloat16), jnp.asarray(spread, jnp.bfloat16))


def body(voltages, fir_taps, station_flags, tile_pairs):
    width = voltages.shape[1]
    taps_count, chans = fir_taps.shape
    local_spectra = voltages.shape[2] // chans
    n_inputs = lax.axis_size("inp")
    n_times = lax.axis_size("tim")
    devices = n_inputs * n_times
    halo = shifted(voltages[:, :, (local_spectra - taps_count + 1) * chans :], "tim", 1)
    flags = jnp.repeat(jnp.repeat(station_flags, 2, axis=0), FLAGRUN, axis=1).astype(jnp.float32)
    spectra = channelize(voltages, halo, fir_taps, flags)
    sectioned = spectra.reshape(devices, chans // devices, 2 * local_spectra, width)
    owned = lax.all_to_all(sectioned, ("inp", "tim"), 0, 0, tiled=True)
    blocks = width * n_inputs // TB
    n_tiles = tile_pairs.shape[0]
    code = tile_pairs[:, 0] * blocks + tile_pairs[:, 1]
    match = jnp.arange(blocks * blocks, dtype=jnp.int32)[:, None] == code[None, :]
    place = jnp.sum(jnp.where(match, jnp.arange(n_tiles, dtype=jnp.int32)[None, :], 0), axis=1)
    out = correlate(owned, place, n_inputs, n_times, n_tiles)
    per_device = chans // devices
    out = out.reshape(per_device, n_tiles, ROWS, 2, LANES)
    return jnp.transpose(out, (0, 1, 3, 2, 4)).reshape(per_device, n_tiles, 2, TB * TB)


def solution(mesh):
    in_specs = (P(None, "inp", "tim"), P(), P("inp", "tim"), P())
    out_specs = P(("inp", "tim"), None, None, None)
    return jax.shard_map(body, mesh=mesh, in_specs=in_specs, out_specs=out_specs, check_vma=False)
```

```python
import functools
import math

import jax
import jax.numpy as jnp
import numpy as np
from jax import lax
from jax.experimental import pallas as pl
from jax.experimental.pallas import tpu as pltpu
from jax.sharding import PartitionSpec as P

TB = 32
FLAGRUN = 4
LANES = 128
PACK = LANES // TB
ROWS = TB // PACK


def shifted(block, axis, distance):
    devices = range(lax.axis_size(axis))
    route = [(i - distance, i) for i in devices if i - distance in devices]
    return lax.ppermute(block, axis, route)


def split_terms(value):
    high = value.astype(jnp.bfloat16)
    return high, (value - high.astype(jnp.float32)).astype(jnp.bfloat16)


def transform_tables(chans):
    radix = chans // LANES
    tables = []
    for q in range(radix):
        phase = np.outer(radix * np.arange(LANES) + q, np.arange(LANES)) % chans
        angle = 2.0 * np.pi * phase / chans
        cosine, sine = np.cos(angle), np.sin(angle)
        real = np.concatenate([cosine, sine], axis=1)
        imag = np.concatenate([-sine, cosine], axis=1)
        tables.append(np.stack([real, imag], axis=1).reshape(2 * LANES, 2 * LANES))
    table = np.stack(tables)
    high = table.astype(jnp.bfloat16)
    low = (table - high.astype(np.float64)).astype(jnp.bfloat16)
    return np.stack([high, low])


def channelize_kernel(*refs, taps, chans, first, count, n_halos, groups, n_started):
    volt_ref = refs[0]
    halo_refs = refs[1 : 1 + n_halos]
    taps_ref, flags_ref, table_ref = refs[1 + n_halos : 4 + n_halos]
    started_refs = refs[4 + n_halos : 4 + n_halos + n_started]
    out_refs = refs[4 + n_halos + n_started :]
    width = volt_ref.shape[1]
    radix = chans // LANES
    scale = 1.0 / (2048.0 * math.sqrt(taps * chans))
    coeffs = taps_ref[...].astype(jnp.float32) * scale

    def frame(part, index):
        ref, slot = volt_ref, index
        for halo_ref in halo_refs:
            if slot < 0:
                ref, slot = halo_ref, slot + halo_ref.shape[2] // chans
        return ref[part, :, slot * chans : (slot + 1) * chans].astype(jnp.float32)

    folded = [[] for _ in range(radix)]
    for s in range(first, first + count):
        flag = flags_ref[:, s : s + 1]
        parts = []
        for part in range(2):
            total = coeffs[0:1] * frame(part, s)
            for p in range(1, taps):
                total = total + coeffs[p : p + 1] * frame(part, s - p)
            total = total * flag
            parts.append([total[:, m * LANES : (m + 1) * LANES] for m in range(radix)])
        (r0, r1, r2, r3), (i0, i1, i2, i3) = parts
        re_even, re_odd, re_diff, re_cross = r0 + r2, r1 + r3, r0 - r2, r1 - r3
        im_even, im_odd, im_diff, im_cross = i0 + i2, i1 + i3, i0 - i2, i1 - i3
        sums = [
            (re_even + re_odd, im_even + im_odd),
            (re_diff + im_cross, im_diff - re_cross),
            (re_even - re_odd, im_even - im_odd),
            (re_diff - im_cross, im_diff + re_cross),
        ]
        for q in range(radix):
            folded[q].append(jnp.concatenate(sums[q], axis=1))
    nt = (((1,), (1,)), ((), ()))
    dot = functools.partial(lax.dot_general, dimension_numbers=nt, preferred_element_type=jnp.float32)
    spread, lanes = out_refs[0].shape[1], width
    for q in range(radix):
        high, low = split_terms(jnp.concatenate(folded[q], axis=0))
        result = dot(table_ref[0, q], high) + (dot(table_ref[1, q], high) + dot(table_ref[0, q], low))
        result = result.astype(jnp.bfloat16)
        owner, slot = divmod(q, radix // spread)
        for out_ref, group in zip(out_refs, groups):
            if 0 <= slot < group:
                for s in range(count):
                    piece = result[:, s * lanes : (s + 1) * lanes]
                    out_ref[:, owner, slot, s] = piece.reshape(out_ref.shape[0], out_ref.shape[4], lanes)
            slot -= group
    for out_ref, started_ref in zip(out_refs, started_refs):
        out_ref[:, :, :, count:] = started_ref[...]


def channel_plan(chans, devices):
    radix = chans // LANES
    per_device = chans // devices
    residues = min(per_device, radix)
    return residues, per_device // residues, radix // residues


def channelize(voltages, halos, fir_taps, flags, first, count, groups, devices, started):
    taps, chans = fir_taps.shape
    width = voltages.shape[1]
    spectra = count + sum(part.shape[3] for part in started[:1])
    _, strip, sharers = channel_plan(chans, devices)
    table = transform_tables(chans)
    return pl.pallas_call(
        functools.partial(
            channelize_kernel,
            taps=taps,
            chans=chans,
            first=first,
            count=count,
            n_halos=len(halos),
            groups=tuple(groups),
            n_started=len(started),
        ),
        out_shape=[
            jax.ShapeDtypeStruct((devices // sharers, sharers, group, spectra, 2 * strip, width), jnp.bfloat16)
            for group in groups
        ],
        compiler_params=pltpu.CompilerParams(vmem_limit_bytes=40 << 20),
        name="channelize",
    )(voltages, *halos, fir_taps, flags, jnp.asarray(table), *started)


def correlate_kernel(*refs, n_inputs, n_times, firsts, begin, residues, n_earlier):
    place_ref = refs[0]
    x_refs = refs[1 : 1 + len(firsts)]
    pick_ref, spread_ref = refs[1 + len(firsts) : 3 + len(firsts)]
    out_ref, rows_ref, *buffers, sems = refs[3 + len(firsts) + n_earlier :]
    slots = [buffers[at : at + 3] for at in range(0, len(buffers), 3)]
    _, group, _, double, width = x_refs[0].shape
    strip = double // 2
    channels = group * strip
    spectra = sum(x_ref.shape[2] for x_ref in x_refs)
    half = n_times * spectra
    depth = 2 * half
    tiles = width // TB
    blocks = n_inputs * tiles
    tall = ROWS * 2
    wide = tiles * LANES
    span = tiles * tall
    zero = jnp.zeros((), jnp.bfloat16)
    lane = lax.broadcasted_iota(jnp.int32, (depth, width), 1) % PACK
    lane_wide = lax.broadcasted_iota(jnp.int32, (depth, wide), 1) // TB % PACK

    def unpack(i):
        for t in range(n_times):
            for x_ref, first in zip(x_refs, firsts):
                for q in range(group):
                    for s in range(x_ref.shape[2]):
                        row = q * strip * depth + t * spectra + first + s
                        value = x_ref[i * n_times + t, q, s].astype(jnp.float32)
                        rows_ref[i, pl.ds(row, double, stride=half), :] = value

    def prepare(channel, slot, i):
        left_ref, right_ref, _ = slots[slot]
        plain = rows_ref[i, pl.ds(pl.multiple_of(channel * depth, depth), depth), :]
        turned = jnp.concatenate([plain[half:], -plain[:half]], axis=0).astype(jnp.bfloat16)
        plain = plain.astype(jnp.bfloat16)
        lefts = [
            jnp.concatenate([jnp.where(lane == u, value, zero) for u in range(PACK)], axis=0)
            for value in (plain, turned)
        ]
        left = lax.dot_general(
            pick_ref[...],
            jnp.concatenate(lefts, axis=1),
            (((1,), (1,)), ((), ())),
            preferred_element_type=jnp.float32,
        )
        left_ref[i * span : (i + 1) * span, :] = left.astype(jnp.bfloat16)
        right = jnp.dot(plain, spread_ref[...], preferred_element_type=jnp.float32).astype(jnp.bfloat16)
        for u in range(PACK):
            right_ref[u * depth : (u + 1) * depth, i * wide : (i + 1) * wide] = jnp.where(
                lane_wide == u, right, zero
            )

    def multiply(slot, pair):
        left_ref, right_ref, tile_ref = slots[slot]
        count = 2 * pair + 2
        grid = jnp.dot(
            left_ref[0 : count * tall, :],
            right_ref[:, pair * 2 * LANES : (pair + 1) * 2 * LANES],
            preferred_element_type=jnp.float32,
        )
        for first in range(count):
            for side in range(2):
                second = 2 * pair + side
                if first <= second:
                    tile_ref[place_ref[first * blocks + second]] = grid[
                        first * tall : (first + 1) * tall, side * LANES : (side + 1) * LANES
                    ]

    def store(channel, slot):
        target = channel % strip * residues + begin + channel // strip
        return pltpu.make_async_copy(slots[slot][2], out_ref.at[target], sems.at[slot])

    for i in range(n_inputs):
        unpack(i)
        prepare(0, 0, i)

    def advance(index, carry):
        for slot in range(len(slots)):
            channel = index * len(slots) + slot
            upcoming = jnp.minimum(channel + 1, channels - 1)

            @pl.when(index > 0)
            def _():
                store(channel - len(slots), slot).wait()

            ahead = [functools.partial(prepare, upcoming, (slot + 1) % len(slots), i) for i in range(n_inputs)]
            pairs = blocks // 2
            if len(slots) == 1 and channels > 1:
                for i in range(n_inputs):
                    prepare(channel, slot, i)
            for pair in range(pairs):
                multiply(slot, pair)
                if len(slots) > 1:
                    for task in ahead[pair * n_inputs // pairs : (pair + 1) * n_inputs // pairs]:
                        task()
            store(channel, slot).start()
        return carry

    rounds = channels // len(slots)
    lax.fori_loop(0, rounds, advance, 0)
    for slot in range(len(slots)):
        store(channels - len(slots) + slot, slot).wait()


def correlate(parts, firsts, place, begin, per_device, residues, n_inputs, n_times, n_tiles, filled):
    _, group, _, double, width = parts[0].shape
    channels = group * double // 2
    total = sum(part.shape[2] for part in parts) * n_times
    tiles = width // TB
    blocks = n_inputs * tiles
    tall = ROWS * 2
    row = np.arange(tiles * tall)
    column = np.arange(width)
    member = (row // 2)[:, None] == (column // PACK)[None, :]
    pick = np.concatenate([member & (row % 2 == q)[:, None] for q in range(2)], axis=1) / total
    lane = np.arange(tiles * LANES)
    spread = (lane // LANES * TB + lane % TB)[None, :] == column[:, None]
    deep = PACK * 2 * total
    earlier = [] if filled is None else [filled]
    slots = 2 if channels % 2 == 0 else 1
    in_vmem = pl.BlockSpec(memory_space=pltpu.VMEM)
    return pl.pallas_call(
        functools.partial(
            correlate_kernel,
            n_inputs=n_inputs,
            n_times=n_times,
            firsts=tuple(firsts),
            begin=begin,
            residues=residues,
            n_earlier=len(earlier),
        ),
        in_specs=[pl.BlockSpec(memory_space=pltpu.SMEM)]
        + [in_vmem] * (len(parts) + 2)
        + [pl.BlockSpec(memory_space=pl.ANY)] * len(earlier),
        out_specs=pl.BlockSpec(memory_space=pl.ANY),
        out_shape=jax.ShapeDtypeStruct((per_device, n_tiles, tall, LANES), jnp.float32),
        scratch_shapes=[pltpu.VMEM((n_inputs, channels * 2 * total, width), jnp.float32)]
        + [
            pltpu.VMEM((blocks * tall, deep), jnp.bfloat16),
            pltpu.VMEM((deep, blocks * LANES), jnp.bfloat16),
            pltpu.VMEM((n_tiles, tall, LANES), jnp.float32),
        ]
        * slots
        + [pltpu.SemaphoreType.DMA((slots,))],
        input_output_aliases={3 + len(parts): 0} if earlier else {},
        compiler_params=pltpu.CompilerParams(vmem_limit_bytes=48 << 20),
        name="correlate",
    )(place, *parts, jnp.asarray(pick, jnp.bfloat16), jnp.asarray(spread, jnp.bfloat16), *earlier)


def body(voltages, fir_taps, station_flags, tile_pairs):
    width = voltages.shape[1]
    taps, chans = fir_taps.shape
    spectra = voltages.shape[2] // chans
    n_inputs = lax.axis_size("inp")
    n_times = lax.axis_size("tim")
    devices = n_inputs * n_times
    per_device = chans // devices
    residues, _, _ = channel_plan(chans, devices)
    halo = shifted(voltages[:, :, (spectra - taps + 1) * chans :], "tim", 1)
    flags = jnp.repeat(jnp.repeat(station_flags, 2, axis=0), FLAGRUN, axis=1).astype(jnp.float32)
    exchange = functools.partial(lax.all_to_all, axis_name=("inp", "tim"), split_axis=0, concat_axis=0, tiled=True)
    groups = [residues // 2, residues - residues // 2] if residues > 1 else [residues]
    blocks = width * n_inputs // TB
    n_tiles = tile_pairs.shape[0]
    code = tile_pairs[:, 0] * blocks + tile_pairs[:, 1]
    match = jnp.arange(blocks * blocks, dtype=jnp.int32)[:, None] == code[None, :]
    place = jnp.sum(jnp.where(match, jnp.arange(n_tiles, dtype=jnp.int32)[None, :], 0), axis=1)
    own = taps - 1
    started = channelize(voltages, [], fir_taps, flags, own, spectra - own, groups, devices, [])
    spectra_groups = channelize(voltages, [halo], fir_taps, flags, 0, own, groups, devices, started)
    owned = [exchange(part.reshape((devices,) + part.shape[2:])) for part in spectra_groups]
    out, begin = None, 0
    for part, group in zip(owned, groups):
        out = correlate([part], [0], place, begin, per_device, residues, n_inputs, n_times, n_tiles, out)
        begin += group
    out = out.reshape(per_device, n_tiles, ROWS, 2, LANES)
    return jnp.transpose(out, (0, 1, 3, 2, 4)).reshape(per_device, n_tiles, 2, TB * TB)


def solution(mesh):
    in_specs = (P(None, "inp", "tim"), P(), P("inp", "tim"), P())
    out_specs = P(("inp", "tim"), None, None, None)
    return jax.shard_map(body, mesh=mesh, in_specs=in_specs, out_specs=out_specs, check_vma=False)
```

```python
import functools
import math

import jax
import jax.numpy as jnp
import numpy as np
from jax import lax
from jax.experimental import pallas as pl
from jax.experimental.pallas import tpu as pltpu
from jax.sharding import PartitionSpec as P

TB = 32
FLAGRUN = 4
LANES = 128
PACK = LANES // TB
ROWS = TB // PACK


def shifted(block, axis, distance):
    devices = range(lax.axis_size(axis))
    route = [(i - distance, i) for i in devices if i - distance in devices]
    return lax.ppermute(block, axis, route)


def split_terms(value):
    high = value.astype(jnp.bfloat16)
    return high, (value - high.astype(jnp.float32)).astype(jnp.bfloat16)


def transform_tables(chans):
    radix = chans // LANES
    tables = []
    for q in range(radix):
        phase = np.outer(radix * np.arange(LANES) + q, np.arange(LANES)) % chans
        angle = 2.0 * np.pi * phase / chans
        cosine, sine = np.cos(angle), np.sin(angle)
        real = np.concatenate([cosine, sine], axis=1)
        imag = np.concatenate([-sine, cosine], axis=1)
        tables.append(np.stack([real, imag], axis=1).reshape(2 * LANES, 2 * LANES))
    table = np.stack(tables)
    high = table.astype(jnp.bfloat16)
    low = (table - high.astype(np.float64)).astype(jnp.bfloat16)
    return np.stack([high, low])


def channelize_kernel(*refs, taps, chans, first, count, n_halos, groups, n_started):
    volt_ref = refs[0]
    halo_refs = refs[1 : 1 + n_halos]
    taps_ref, flags_ref, table_ref = refs[1 + n_halos : 4 + n_halos]
    started_refs = refs[4 + n_halos : 4 + n_halos + n_started]
    out_refs = refs[4 + n_halos + n_started :]
    width = volt_ref.shape[1]
    radix = chans // LANES
    scale = 1.0 / (2048.0 * math.sqrt(taps * chans))
    coeffs = taps_ref[...].astype(jnp.float32) * scale

    def frame(part, index):
        ref, slot = volt_ref, index
        for halo_ref in halo_refs:
            if slot < 0:
                ref, slot = halo_ref, slot + halo_ref.shape[2] // chans
        return ref[part, :, slot * chans : (slot + 1) * chans].astype(jnp.float32)

    folded = [[] for _ in range(radix)]
    for s in range(first, first + count):
        flag = flags_ref[:, s : s + 1]
        parts = []
        for part in range(2):
            total = coeffs[0:1] * frame(part, s)
            for p in range(1, taps):
                total = total + coeffs[p : p + 1] * frame(part, s - p)
            total = total * flag
            parts.append([total[:, m * LANES : (m + 1) * LANES] for m in range(radix)])
        (r0, r1, r2, r3), (i0, i1, i2, i3) = parts
        re_even, re_odd, re_diff, re_cross = r0 + r2, r1 + r3, r0 - r2, r1 - r3
        im_even, im_odd, im_diff, im_cross = i0 + i2, i1 + i3, i0 - i2, i1 - i3
        sums = [
            (re_even + re_odd, im_even + im_odd),
            (re_diff + im_cross, im_diff - re_cross),
            (re_even - re_odd, im_even - im_odd),
            (re_diff - im_cross, im_diff + re_cross),
        ]
        for q in range(radix):
            folded[q].append(jnp.concatenate(sums[q], axis=1))
    nt = (((1,), (1,)), ((), ()))
    dot = functools.partial(lax.dot_general, dimension_numbers=nt, preferred_element_type=jnp.float32)
    spread, lanes = out_refs[0].shape[1], width
    for q in range(radix):
        high, low = split_terms(jnp.concatenate(folded[q], axis=0))
        result = dot(table_ref[0, q], high) + (dot(table_ref[1, q], high) + dot(table_ref[0, q], low))
        result = result.astype(jnp.bfloat16)
        owner, slot = divmod(q, radix // spread)
        for out_ref, group in zip(out_refs, groups):
            if 0 <= slot < group:
                for s in range(count):
                    piece = result[:, s * lanes : (s + 1) * lanes]
                    out_ref[:, owner, slot, s] = piece.reshape(out_ref.shape[0], out_ref.shape[4], lanes)
            slot -= group
    for out_ref, started_ref in zip(out_refs, started_refs):
        out_ref[:, :, :, count:] = started_ref[...]


def channel_plan(chans, devices):
    radix = chans // LANES
    per_device = chans // devices
    residues = min(per_device, radix)
    return residues, per_device // residues, radix // residues


def channelize(voltages, halos, fir_taps, flags, first, count, groups, devices, started):
    taps, chans = fir_taps.shape
    width = voltages.shape[1]
    spectra = count + sum(part.shape[3] for part in started[:1])
    _, strip, sharers = channel_plan(chans, devices)
    table = transform_tables(chans)
    return pl.pallas_call(
        functools.partial(
            channelize_kernel,
            taps=taps,
            chans=chans,
            first=first,
            count=count,
            n_halos=len(halos),
            groups=tuple(groups),
            n_started=len(started),
        ),
        out_shape=[
            jax.ShapeDtypeStruct((devices // sharers, sharers, group, spectra, 2 * strip, width), jnp.bfloat16)
            for group in groups
        ],
        compiler_params=pltpu.CompilerParams(vmem_limit_bytes=16 << 20),
        name="channelize",
    )(voltages, *halos, fir_taps, flags, jnp.asarray(table), *started)


def correlate_kernel(*refs, n_inputs, n_times, firsts, begin, residues, n_earlier):
    place_ref = refs[0]
    x_refs = refs[1 : 1 + len(firsts)]
    pick_ref, spread_ref = refs[1 + len(firsts) : 3 + len(firsts)]
    out_ref, rows_ref, *buffers, sems = refs[3 + len(firsts) + n_earlier :]
    slots = [buffers[at : at + 3] for at in range(0, len(buffers), 3)]
    _, group, _, double, width = x_refs[0].shape
    strip = double // 2
    channels = group * strip
    spectra = sum(x_ref.shape[2] for x_ref in x_refs)
    half = n_times * spectra
    depth = 2 * half
    tiles = width // TB
    blocks = n_inputs * tiles
    tall = ROWS * 2
    wide = tiles * LANES
    span = tiles * tall
    zero = jnp.zeros((), jnp.bfloat16)
    lane = lax.broadcasted_iota(jnp.int32, (depth, width), 1) % PACK
    lane_pair = lax.broadcasted_iota(jnp.int32, (depth, 2 * LANES), 1) // TB % PACK

    def unpack(i, residues_now):
        for t in range(n_times):
            for x_ref, first in zip(x_refs, firsts):
                for q in residues_now:
                    for s in range(x_ref.shape[2]):
                        row = q * strip * depth + t * spectra + first + s
                        value = x_ref[i * n_times + t, q, s].astype(jnp.float32)
                        rows_ref[i, pl.ds(row, double, stride=half), :] = value

    def prepare(channel, slot, i):
        left_ref, right_ref, _ = slots[slot]
        plain = rows_ref[i, pl.ds(pl.multiple_of(channel * depth, depth), depth), :]
        turned = jnp.concatenate([plain[half:], -plain[:half]], axis=0).astype(jnp.bfloat16)
        plain = plain.astype(jnp.bfloat16)
        lefts = [
            jnp.concatenate([jnp.where(lane == u, value, zero) for u in range(PACK)], axis=0)
            for value in (plain, turned)
        ]
        left = lax.dot_general(
            pick_ref[...],
            jnp.concatenate(lefts, axis=1),
            (((1,), (1,)), ((), ())),
            preferred_element_type=jnp.float32,
        )
        left_ref[i * span : (i + 1) * span, :] = left.astype(jnp.bfloat16)
        right = jnp.dot(plain, spread_ref[...], preferred_element_type=jnp.float32)
        right_ref[:, i * wide : (i + 1) * wide] = right.astype(jnp.bfloat16)

    def multiply(slot, pair):
        left_ref, right_ref, tile_ref = slots[slot]
        count = 2 * pair + 2
        right = right_ref[:, pair * 2 * LANES : (pair + 1) * 2 * LANES]
        grid = jnp.dot(
            left_ref[0 : count * tall, :],
            jnp.concatenate([jnp.where(lane_pair == u, right, zero) for u in range(PACK)], axis=0),
            preferred_element_type=jnp.float32,
        )
        for first in range(count):
            for side in range(2):
                second = 2 * pair + side
                if first <= second:
                    tile_ref[place_ref[first * blocks + second]] = grid[
                        first * tall : (first + 1) * tall, side * LANES : (side + 1) * LANES
                    ]

    def store(channel, slot):
        target = channel % strip * residues + begin + channel // strip
        return pltpu.make_async_copy(slots[slot][2], out_ref.at[target], sems.at[slot])

    now = 1 if strip > 1 else group
    for i in range(n_inputs):
        unpack(i, range(now))
        prepare(0, 0, i)

    def advance(index, carry):
        for slot in range(len(slots)):
            channel = index * len(slots) + slot
            upcoming = jnp.minimum(channel + 1, channels - 1)

            @pl.when(index > 0)
            def _():
                store(channel - len(slots), slot).wait()

            ahead = [functools.partial(prepare, upcoming, (slot + 1) % len(slots), i) for i in range(n_inputs)]
            pairs = blocks // 2
            if len(slots) == 1 and channels > 1:
                for i in range(n_inputs):
                    prepare(channel, slot, i)
            for pair in range(pairs):
                multiply(slot, pair)
            store(channel, slot).start()
            if len(slots) > 1:
                for task in ahead:
                    task()
            if slot == 0 and now < group:

                @pl.when(index == 0)
                def _():
                    for i in range(n_inputs):
                        unpack(i, range(now, group))

        return carry

    rounds = channels // len(slots)
    lax.fori_loop(0, rounds, advance, 0)
    for slot in range(len(slots)):
        store(channels - len(slots) + slot, slot).wait()


def correlate(parts, firsts, place, begin, per_device, residues, n_inputs, n_times, n_tiles, filled):
    _, group, _, double, width = parts[0].shape
    channels = group * double // 2
    total = sum(part.shape[2] for part in parts) * n_times
    tiles = width // TB
    blocks = n_inputs * tiles
    tall = ROWS * 2
    row = np.arange(tiles * tall)
    column = np.arange(width)
    member = (row // 2)[:, None] == (column // PACK)[None, :]
    pick = np.concatenate([member & (row % 2 == q)[:, None] for q in range(2)], axis=1) / total
    lane = np.arange(tiles * LANES)
    spread = (lane // LANES * TB + lane % TB)[None, :] == column[:, None]
    deep = PACK * 2 * total
    earlier = [] if filled is None else [filled]
    slots = 2 if channels % 2 == 0 else 1
    in_vmem = pl.BlockSpec(memory_space=pltpu.VMEM)
    return pl.pallas_call(
        functools.partial(
            correlate_kernel,
            n_inputs=n_inputs,
            n_times=n_times,
            firsts=tuple(firsts),
            begin=begin,
            residues=residues,
            n_earlier=len(earlier),
        ),
        in_specs=[pl.BlockSpec(memory_space=pltpu.SMEM)]
        + [in_vmem] * (len(parts) + 2)
        + [pl.BlockSpec(memory_space=pl.ANY)] * len(earlier),
        out_specs=pl.BlockSpec(memory_space=pl.ANY),
        out_shape=jax.ShapeDtypeStruct((per_device, n_tiles, tall, LANES), jnp.float32),
        scratch_shapes=[pltpu.VMEM((n_inputs, channels * 2 * total, width), jnp.float32)]
        + [
            pltpu.VMEM((blocks * tall, deep), jnp.bfloat16),
            pltpu.VMEM((2 * total, blocks * LANES), jnp.bfloat16),
            pltpu.VMEM((n_tiles, tall, LANES), jnp.float32),
        ]
        * slots
        + [pltpu.SemaphoreType.DMA((slots,))],
        input_output_aliases={3 + len(parts): 0} if earlier else {},
        compiler_params=pltpu.CompilerParams(vmem_limit_bytes=24 << 20),
        name="correlate",
    )(place, *parts, jnp.asarray(pick, jnp.bfloat16), jnp.asarray(spread, jnp.bfloat16), *earlier)


def body(voltages, fir_taps, station_flags, tile_pairs):
    width = voltages.shape[1]
    taps, chans = fir_taps.shape
    spectra = voltages.shape[2] // chans
    n_inputs = lax.axis_size("inp")
    n_times = lax.axis_size("tim")
    devices = n_inputs * n_times
    per_device = chans // devices
    residues, _, _ = channel_plan(chans, devices)
    halo = shifted(voltages[:, :, (spectra - taps + 1) * chans :], "tim", 1)
    flags = jnp.repeat(jnp.repeat(station_flags, 2, axis=0), FLAGRUN, axis=1).astype(jnp.float32)
    exchange = functools.partial(lax.all_to_all, axis_name=("inp", "tim"), split_axis=0, concat_axis=0, tiled=True)
    groups = [residues // 2, residues - residues // 2] if residues > 1 else [residues]
    blocks = width * n_inputs // TB
    n_tiles = tile_pairs.shape[0]
    code = tile_pairs[:, 0] * blocks + tile_pairs[:, 1]
    match = jnp.arange(blocks * blocks, dtype=jnp.int32)[:, None] == code[None, :]
    place = jnp.sum(jnp.where(match, jnp.arange(n_tiles, dtype=jnp.int32)[None, :], 0), axis=1)
    halo, place = lax.optimization_barrier((halo, place))
    own = taps - 1
    started = channelize(voltages, [], fir_taps, flags, own, spectra - own, groups, devices, [])
    spectra_groups = channelize(voltages, [halo], fir_taps, flags, 0, own, groups, devices, started)
    owned = [exchange(part.reshape((devices,) + part.shape[2:])) for part in spectra_groups]
    out, begin = None, 0
    for part, group in zip(owned, groups):
        out = correlate([part], [0], place, begin, per_device, residues, n_inputs, n_times, n_tiles, out)
        begin += group
    out = out.reshape(per_device, n_tiles, ROWS, 2, LANES)
    return jnp.transpose(out, (0, 1, 3, 2, 4)).reshape(per_device, n_tiles, 2, TB * TB)


def solution(mesh):
    in_specs = (P(None, "inp", "tim"), P(), P("inp", "tim"), P())
    out_specs = P(("inp", "tim"), None, None, None)
    return jax.shard_map(body, mesh=mesh, in_specs=in_specs, out_specs=out_specs, check_vma=False)
```
